256 devices in a mesh: grp: 8 (over x, core), dev: 32 (over z, y).
Axes of the slice: x: 4, y: 4, z: 8, core: 2. Of those that a mesh axis runs over, the one named last changes fastest.
Arguments:
- ladder_amps: bfloat16 [64, 144, 4096], P('dev', 'grp'), may hold values from -6 to 6
- ladder_ids: int32 [64, 144], P('dev', 'grp'), may hold values from 0 to 23, as said below
- ladder_count: int32 [64, 8], P('dev', 'grp'), may hold values from 9 to 18, as said below
- cycle_amps: bfloat16 [64, 48, 4096], P('dev', 'grp'), may hold values from -6 to 6
- cycle_ids: int32 [64, 48], P('dev', 'grp'), may hold values from 0 to 7, as said below
- cycle_count: int32 [64, 8], P('dev', 'grp'), may hold values from 3 to 6, as said below
- ladder_panel: bfloat16 [12288, 16384], P('grp', 'dev'), may hold values from -0.0546875 to 0.0546875
- cycle_panel: bfloat16 [4096, 16384], P('grp', 'dev'), may hold values from -0.09375 to 0.09375
- owners: int32 [64], replicated, may hold values from 0 to 63, each once
- base: float32 [4096, 16384], P('grp', 'dev'), may hold values from -6 to 6
Outputs:
- residual: float32 [4096, 16384], P('grp', 'dev')
The draws below stay inside these ranges and needn't reach their ends.
Inputs may be any that keep to these rules, and one draw needn't show every extreme that they name: `ladder_ids`: within one row tile and group the slots name distinct tiles of 0 to 23. `cycle_ids`: within one row tile and group the slots name distinct tiles of 0 to 7. `ladder_count`: slots at or past the count are not live; in every group some row tile has all 18 slots live. `cycle_count`: slots at or past the count are not live; in every group some row tile has all 6 slots live.
All inputs are finite; a program needn't handle non-finite values.
Results may differ from the reference program's by a relative error of at most 0.0003.
Values may be sent and summed in bfloat16 or wider, within the bound.
A program may use at most 128 MiB of HBM per device.

```python
import jax
import jax.numpy as jnp
from jax import lax

TS = 64
KLT = 24
KRT = 8
KCAP_L = 18
KCAP_R = 6
ROW_TILES = 64
ROWS = 4096
COLS = 16384
KL_ROWS = 12288
KR_ROWS = 4096
L_SLOTS = 144
R_SLOTS = 48
N_GRP = 8


def tile_lists(key, ktiles, cap):
    scores = jax.random.randint(key, (ROW_TILES, N_GRP, ktiles), 0, 1 << 20) * ktiles
    scores = scores + jnp.arange(ktiles, dtype=jnp.int32)[None, None, :]
    order = jnp.argsort(scores, axis=-1, stable=True)
    return order[:, :, :cap].reshape(ROW_TILES, N_GRP * cap).astype(jnp.int32)


def slot_counts(key, cap):
    first_key, second_key = jax.random.split(key)
    lower = (cap + 1) // 2
    counts = jax.random.randint(first_key, (ROW_TILES, N_GRP), lower, cap + 1)
    chosen = jax.random.randint(second_key, (1, N_GRP), 0, ROW_TILES)
    full_row = jnp.arange(ROW_TILES, dtype=jnp.int32)[:, None] == chosen
    return jnp.where(full_row, cap, counts).astype(jnp.int32)


def draw_ladder_ids(key, part):
    return tile_lists(jax.random.fold_in(key, 11), KLT, KCAP_L)


def draw_cycle_ids(key, part):
    return tile_lists(jax.random.fold_in(key, 23), KRT, KCAP_R)


def draw_ladder_count(key, part):
    return slot_counts(jax.random.fold_in(key, 37), KCAP_L)


def draw_cycle_count(key, part):
    return slot_counts(jax.random.fold_in(key, 41), KCAP_R)


def steps_of(key, extent, cuts, least, largest):
    def one(axis_at, shards_of):
        draws = jax.random.uniform(jax.random.fold_in(jax.random.fold_in(key, 6), axis_at), (shards_of,), jnp.float32, least / len(cuts), largest / len(cuts))
        return jnp.repeat(jnp.exp(draws), extent[axis_at] // shards_of).reshape((-1,) + (1,) * (len(extent) - axis_at - 1))

    loudness = one(*cuts[0])
    for cut in cuts[1:]:
        loudness = loudness * one(*cut)
    return loudness


def centred(own_key, dims, width, reach, cuts=(), held_as=jnp.bfloat16):
    gain = steps_of(own_key, dims, cuts, -0.22, 0.18) if cuts else 1.0
    drawn = jax.random.normal(own_key, dims, jnp.float32) * width * gain
    return jnp.minimum(jnp.maximum(drawn, -reach), reach).astype(held_as)


def setup_inputs(seed: int = 0) -> dict:
    arg_keys = jax.random.split(jax.random.key(seed), 11)
    ladder_amps = centred(arg_keys[0], (ROW_TILES, L_SLOTS, TS * TS), 1.0, 6.0, ((0, 32), (1, 8)))
    ladder_ids = draw_ladder_ids(jax.random.fold_in(arg_keys[10], 71), 0)
    ladder_count = draw_ladder_count(jax.random.fold_in(arg_keys[10], 71), 0)
    cycle_amps = centred(arg_keys[3], (ROW_TILES, R_SLOTS, TS * TS), 1.0, 6.0, ((0, 32), (1, 8)))
    cycle_ids = draw_cycle_ids(jax.random.fold_in(arg_keys[10], 71), 0)
    cycle_count = draw_cycle_count(jax.random.fold_in(arg_keys[10], 71), 0)
    ladder_panel = centred(arg_keys[6], (KL_ROWS, COLS), KL_ROWS ** -0.5, 0.0546875, ((0, 8), (1, 32)))
    cycle_panel = centred(arg_keys[7], (KR_ROWS, COLS), KR_ROWS ** -0.5, 0.09375, ((0, 8), (1, 32)))
    owners = jax.random.permutation(arg_keys[8], ROW_TILES).astype(jnp.int32)
    base = centred(arg_keys[9], (ROWS, COLS), 1.0, 6.0, ((0, 8), (1, 32)), jnp.float32)
    return {"ladder_amps": ladder_amps, "ladder_ids": ladder_ids, "ladder_count": ladder_count, "cycle_amps": cycle_amps, "cycle_ids": cycle_ids, "cycle_count": cycle_count, "ladder_panel": ladder_panel, "cycle_panel": cycle_panel, "owners": owners, "base": base}


def place_tiles(amps, ids, count, group, cap, ktiles):
    block = lax.dynamic_slice_in_dim(amps, group * cap, cap, 1)
    slots = lax.dynamic_slice_in_dim(ids, group * cap, cap, 1)
    filled = lax.dynamic_slice_in_dim(count, group, 1, 1)
    live_slots = (jnp.arange(cap, dtype=jnp.int32)[None, :] < filled).astype(jnp.float32)
    onehot = (slots[:, :, None] == jnp.arange(ktiles, dtype=jnp.int32)[None, None, :]).astype(jnp.float32)
    onehot = onehot * live_slots[:, :, None]
    tiles = block.astype(jnp.float32).reshape(ROW_TILES, cap, TS, TS)
    dense = jnp.einsum("rjk,rjab->rakb", onehot, tiles)
    return dense.reshape(ROW_TILES * TS, ktiles * TS).astype(jnp.bfloat16)


def reference(ladder_amps, ladder_ids, ladder_count, cycle_amps, cycle_ids, cycle_count, ladder_panel, cycle_panel, owners, base):
    def add_group(total, group):
        ladder_dense = place_tiles(ladder_amps, ladder_ids, ladder_count, group, KCAP_L, KLT)
        cycle_dense = place_tiles(cycle_amps, cycle_ids, cycle_count, group, KCAP_R, KRT)
        ladder_rows = lax.dynamic_slice_in_dim(ladder_panel, group * (KLT * TS), KLT * TS, 0)
        cycle_rows = lax.dynamic_slice_in_dim(cycle_panel, group * (KRT * TS), KRT * TS, 0)
        part_sum = jnp.dot(ladder_dense, ladder_rows, preferred_element_type=jnp.float32)
        part_sum = part_sum + jnp.dot(cycle_dense, cycle_rows, preferred_element_type=jnp.float32)
        return total + part_sum, None

    start_total = jnp.zeros((ROWS, COLS), jnp.float32)
    total, _ = lax.scan(add_group, start_total, jnp.arange(N_GRP, dtype=jnp.int32))
    ordered = total.reshape(ROW_TILES, TS, COLS)[owners].reshape(ROWS, COLS)
    return base + ordered
```

```python
import jax
import jax.numpy as jnp
from jax import lax
from jax.experimental import pallas as pl
from jax.experimental.pallas import tpu as pltpu
from jax.sharding import PartitionSpec as P

TS = 64
KLT = 24
KRT = 8
MESH = pl.DeviceIdType.MESH
STEPS = 16
PAIRS = 12
HALF = 32
ZERO = PAIRS
VAR = PAIRS + 1


def pos_first(z, y):
    return 4 * z + (y + z) % 4


def dev_first(s):
    k = s // 4
    return 4 * k + (s % 4 + 32 - k) % 4


def pos_second(z, y):
    t = (z + 24 - 3 * y) % 8
    return 4 * y + 16 * (t // 4) + t % 4


def dev_second(s):
    k = s // 4
    return 4 * ((3 * k + s % 4) % 8) + k % 4


POS = (pos_first, pos_second)
DEV = (dev_first, dev_second)


def kernel(
    own, tab_in, loc, lad, cyc, out,
    held, tab_v, tab_s, panel, spread, lhs, part, got, total, fin_s, fin_r,
    local_sem, pair_s, pair_r, tab_ss, tab_rs, ring_s, ring_r, red_s, red_r, sh_s, sh_r, fin_ss, fin_rs,
):
    g = lax.axis_index("grp")
    d = lax.axis_index("dev")
    x = g // 2
    c = g % 2
    z = d // 4
    y = d % 4
    other = 1 - c
    mate = (2 * x + other, d)
    pos = [POS[h](z, y) for h in range(2)]
    nxt = [(g, DEV[h]((pos[h] + 1) % 32)) for h in range(2)]
    prv = [(g, DEV[h]((pos[h] + 31) % 32)) for h in range(2)]

    def local(i, src, dst):
        return pltpu.make_async_copy(src, dst, local_sem.at[i])

    def to_mate(i, src, dst):
        return pltpu.make_async_remote_copy(
            src_ref=src, dst_ref=dst, send_sem=pair_s.at[i], recv_sem=pair_r.at[i],
            device_id=mate, device_id_type=MESH)

    locals_ = [
        local(0, own.at[c, 0], held.at[0, 0, c]),
        local(1, own.at[c, 1], held.at[1, 0, c]),
        local(2, tab_in.at[c], tab_v.at[d, c]),
        local(3, lad, panel.at[c, pl.ds(0, 1536)]),
        local(4, cyc, panel.at[c, pl.ds(1536, 512)]),
    ]

    def mates(side):
        return [
            to_mate(0, own.at[other, 0], held.at[0, 0, side]),
            to_mate(1, own.at[other, 1], held.at[1, 0, side]),
            to_mate(2, tab_in.at[other], tab_v.at[d, side]),
            to_mate(3, lad, panel.at[side, pl.ds(0, 1536)]),
            to_mate(4, cyc, panel.at[side, pl.ds(1536, 512)]),
        ]

    going = mates(c)
    coming = mates(other)
    for i in range(5):
        locals_[i].start()
        going[i].start()

    def hop(h, up, src, dst, kg):
        return pltpu.make_async_remote_copy(
            src_ref=held.at[h, src, kg], dst_ref=held.at[h, dst, kg],
            send_sem=ring_s.at[h, dst, kg], recv_sem=ring_r.at[h, dst, kg],
            device_id=nxt[h] if up else prv[h], device_id_type=MESH)

    for h in range(2):
        locals_[h].wait()
    for h in range(2):
        coming[h].wait_recv()
    for kg in range(2):
        for h in range(2):
            hop(h, True, 0, 1, kg).start()
            hop(h, False, 0, 31, kg).start()

    locals_[2].wait()
    coming[2].wait_recv()

    def table_to(i):
        return pltpu.make_async_remote_copy(
            src_ref=tab_v.at[d], dst_ref=tab_v.at[d], send_sem=tab_ss, recv_sem=tab_rs,
            device_id=(g, (d + i) % 32), device_id_type=MESH)

    @pl.loop(1, 32)
    def _(i):
        table_to(i).start()

    spread[ZERO] = jnp.zeros((HALF, 128), jnp.bfloat16)
    spread[VAR + ZERO] = jnp.zeros((HALF, 128), jnp.bfloat16)

    every = tab_v.at[pl.ds(0, 31)]
    pltpu.make_async_copy(every, every, tab_rs).wait()
    pltpu.make_async_copy(every, every, tab_ss).wait()
    to_smem = pltpu.make_async_copy(tab_v, tab_s, local_sem.at[5])
    to_smem.start()
    for i in (3, 4):
        locals_[i].wait()
        coming[i].wait_recv()
    to_smem.wait()

    left = lax.broadcasted_iota(jnp.int32, (HALF, 128), 1) < 64

    def reduce_copy(b, r):
        to = (x + r) % 4
        return pltpu.make_async_remote_copy(
            src_ref=part.at[b, to], dst_ref=got.at[b, r - 1],
            send_sem=red_s.at[b, r - 1], recv_sem=red_r.at[b, r - 1],
            device_id=(2 * to + c, d), device_id_type=MESH)

    def share_copy(b, side):
        rows = total.at[pl.ds((side * STEPS + b) * 4, 4)]
        return pltpu.make_async_remote_copy(
            src_ref=rows, dst_ref=rows, send_sem=sh_s.at[b], recv_sem=sh_r.at[b],
            device_id=mate, device_id_type=MESH)

    def finish(b):
        for r in (1, 2, 3):
            reduce_copy(b, r).wait_recv()
        s = part[b, x] + got[b, 0] + got[b, 1] + got[b, 2]
        for q in range(4):
            total[(c * STEPS + b) * 4 + q] = s[HALF * q:HALF * (q + 1)]
        share_copy(b, c).start()

    @pl.loop(0, STEPS)
    def _(b):
        for kg in range(2):
            for h in range(2):
                @pl.when(b < 15)
                def _():
                    hop(h, True, b, b + 1, kg).wait_recv()

                @pl.when(b < 14)
                def _():
                    hop(h, True, b + 1, b + 2, kg).start()

                hop(h, False, 0, 31 - b, kg).wait_recv()

                @pl.when(b < 15)
                def _():
                    hop(h, False, 31 - b, 30 - b, kg).start()

            for q in range(4):
                h = q // 2
                m = b if q % 2 == 0 else 31 - b
                src = DEV[h]((pos[h] + 32 - m) % 32)
                for p in range(PAIRS):
                    v = held[h, m, kg, p]
                    spread[p] = v
                    spread[VAR + p] = jnp.concatenate([v[:, 64:], v[:, :64]], axis=1)
                for j in range(16):
                    a = tab_s[src, kg, 0, 2 * j]
                    e = tab_s[src, kg, 0, 2 * j + 1]
                    lhs[HALF * q:HALF * (q + 1), 128 * j:128 * (j + 1)] = jnp.where(left, spread[a], spread[e])
            prod = jnp.dot(lhs[...], panel[kg], preferred_element_type=jnp.float32)
            for q in range(4):
                piece = prod[:, 128 * q:128 * (q + 1)]
                part[b, q] = piece if kg == 0 else part[b, q] + piece
        for r in (2, 1, 3):
            reduce_copy(b, r).start()

        @pl.when(b >= 2)
        def _():
            finish(b - 2)

    finish(STEPS - 2)
    finish(STEPS - 1)

    @pl.loop(0, STEPS)
    def _(b):
        share_copy(b, other).wait_recv()

    def final_copy(r):
        to = (x + r) % 4
        return pltpu.make_async_remote_copy(
            src_ref=fin_s.at[r], dst_ref=fin_r.at[r - 1], send_sem=fin_ss.at[r - 1], recv_sem=fin_rs.at[r - 1],
            device_id=(2 * to + c, d), device_id_type=MESH)

    for r in (2, 1, 3, 0):
        to = (x + r) % 4
        for i in range(16):
            fin_s[r, HALF * i:HALF * (i + 1)] = total[loc[to * 16 + i]]
        if r:
            final_copy(r).start()
    out[x] = fin_s[0]
    for r in (1, 3, 2):
        final_copy(r).wait_recv()
        out[(x + 4 - r) % 4] = fin_r[r - 1]

    for i in range(5):
        going[i].wait_send()
    for r in (1, 2, 3):
        final_copy(r).wait_send()

    @pl.loop(0, STEPS)
    def _(b):
        share_copy(b, c).wait_send()
        for r in (1, 2, 3):
            reduce_copy(b, r).wait_send()
        for kg in range(2):
            for h in range(2):
                @pl.when(b < 15)
                def _():
                    hop(h, True, b, b + 1, kg).wait_send()
                hop(h, False, 0, 31 - b, kg).wait_send()


def per_device(
    ladder_amps, ladder_ids, ladder_count, cycle_amps, cycle_ids, cycle_count,
    ladder_panel, cycle_panel, owners, base,
):
    i32 = jnp.int32
    amps = jnp.concatenate([ladder_amps, cycle_amps], axis=1)
    own = amps.reshape(2, PAIRS, 2, 2, HALF, TS).transpose(0, 3, 1, 4, 2, 5).reshape(2, 2, PAIRS, HALF, 128)

    ids = jnp.concatenate([ladder_ids, cycle_ids + KLT], axis=1)
    nl, nc = ladder_ids.shape[1], cycle_ids.shape[1]
    slot = jnp.arange(nl + nc, dtype=i32)
    live = jnp.where(slot < nl, slot[None] < ladder_count, slot[None] - nl < cycle_count)
    code = VAR * ((slot & 1)[None] ^ (ids & 1)) + (slot // 2)[None] - ZERO
    hit = (ids[:, :, None] == jnp.arange(128, dtype=i32)) & live[:, :, None]
    table = ZERO + jnp.sum(jnp.where(hit, code[:, :, None], 0), axis=1, dtype=i32)
    table = table.reshape(2, 1, 128)

    g = lax.axis_index("grp")
    d = lax.axis_index("dev")
    c, z, y = g % 2, d // 4, d % 4
    tiles = owners.reshape(4, 2, 8)[:, c]
    src = tiles // 2
    spots = []
    for h in range(2):
        m = (POS[h](z, y) + 32 - POS[h](src // 4, src % 4)) % 32
        far = (m >= STEPS).astype(i32)
        b = jnp.where(m >= STEPS, 31 - m, m)
        spots.append((tiles % 2 * STEPS + b) * 4 + 2 * h + far)
    loc = jnp.stack(spots, axis=-1).reshape(64)

    hbm = pl.BlockSpec(memory_space=pl.ANY)
    bf16, f32 = jnp.bfloat16, jnp.float32
    dma = pltpu.SemaphoreType.DMA
    summed = pl.pallas_call(
        kernel,
        name="ladder_ring",
        out_shape=jax.ShapeDtypeStruct((4, 512, 128), f32),
        in_specs=[hbm, hbm, pl.BlockSpec(memory_space=pltpu.SMEM), hbm, hbm],
        out_specs=pl.BlockSpec(memory_space=pltpu.VMEM),
        scratch_shapes=[
            pltpu.VMEM((2, 32, 2, PAIRS, HALF, 128), bf16),
            pltpu.VMEM((32, 2, 1, 128), i32),
            pltpu.SMEM((32, 2, 1, 128), i32),
            pltpu.VMEM((2, 2048, 512), bf16),
            pltpu.VMEM((2 * VAR, HALF, 128), bf16),
            pltpu.VMEM((128, 2048), bf16),
            pltpu.VMEM((STEPS, 4, 128, 128), f32),
            pltpu.VMEM((STEPS, 3, 128, 128), f32),
            pltpu.VMEM((2 * STEPS * 4, HALF, 128), f32),
            pltpu.VMEM((4, 512, 128), f32),
            pltpu.VMEM((3, 512, 128), f32),
            dma((6,)), dma((5,)), dma((5,)), dma, dma,
            dma((2, 32, 2)), dma((2, 32, 2)),
            dma((STEPS, 3)), dma((STEPS, 3)), dma((STEPS,)), dma((STEPS,)),
            dma((3,)), dma((3,)),
        ],
        compiler_params=pltpu.CompilerParams(has_side_effects=True, vmem_limit_bytes=58 * 2**20),
    )(own, table, loc, ladder_panel, cycle_panel)
    return base + summed.transpose(1, 0, 2).reshape(512, 512)


def solution(mesh):
    placed = (
        P("dev", "grp", None),
        P("dev", "grp"),
        P("dev", "grp"),
        P("dev", "grp", None),
        P("dev", "grp"),
        P("dev", "grp"),
        P("grp", "dev"),
        P("grp", "dev"),
        P(),
        P("grp", "dev"),
    )
    return jax.shard_map(
        per_device, mesh=mesh, in_specs=placed, out_specs=P("grp", "dev"), check_vma=False
    )
```

```python
import jax
import jax.numpy as jnp
from jax import lax
from jax.experimental import pallas as pl
from jax.experimental.pallas import tpu as pltpu
from jax.sharding import PartitionSpec as P

TS = 64
KLT = 24
KRT = 8
MESH = pl.DeviceIdType.MESH
STEPS = 16
PAIRS = 12
HALF = 32
KCAP_L = 18
KCAP_R = 6
CUTS = 2
CUT = PAIRS // CUTS
ZERO = PAIRS
VAR = PAIRS + 1


def pos_first(z, y):
    return 4 * z + (y + z) % 4


def dev_first(s):
    k = s // 4
    return 4 * k + (s % 4 + 32 - k) % 4


def pos_second(z, y):
    t = (z + 24 - 3 * y) % 8
    return 4 * y + 16 * (t // 4) + t % 4


def dev_second(s):
    k = s // 4
    return 4 * ((3 * k + s % 4) % 8) + k % 4


POS = (pos_first, pos_second)
DEV = (dev_first, dev_second)


def kernel(
    own, lad_ids, lad_n, cyc_ids, cyc_n, owners, lad, cyc, out,
    held, tab_own, tab_v, tab_s, loc, panel, spread, lhs, part, got, total, fin_s, fin_r,
    local_sem, pair_s, pair_r, tab_ss, tab_rs, tab_ls, ring_s, ring_r,
    red_s, red_r, sh_s, sh_r, fin_ss, fin_rs,
):
    g = lax.axis_index("grp")
    d = lax.axis_index("dev")
    x = g // 2
    c = g % 2
    z = d // 4
    y = d % 4
    other = 1 - c
    mate = (2 * x + other, d)
    pos = [POS[h](z, y) for h in range(2)]
    nxt = [(g, DEV[h]((pos[h] + 1) % 32)) for h in range(2)]
    prv = [(g, DEV[h]((pos[h] + 31) % 32)) for h in range(2)]

    def local(i, src, dst):
        return pltpu.make_async_copy(src, dst, local_sem.at[i])

    def to_mate(i, src, dst):
        return pltpu.make_async_remote_copy(
            src_ref=src, dst_ref=dst, send_sem=pair_s.at[i], recv_sem=pair_r.at[i],
            device_id=mate, device_id_type=MESH)

    own_here = [local(h, own.at[c, h], held.at[h, 0, c]) for h in range(2)]
    panels_here = [
        local(2, lad, panel.at[c, pl.ds(0, 1536)]),
        local(3, cyc, panel.at[c, pl.ds(1536, 512)]),
    ]
    for copy in own_here + panels_here:
        copy.start()

    barrier = pltpu.get_barrier_semaphore()
    peers = nxt + prv + [mate] + [(2 * ((x + r) % 4) + c, d) for r in (1, 2, 3)]
    for p in peers:
        pl.semaphore_signal(barrier, inc=1, device_id=p, device_id_type=MESH)

    lane = lax.broadcasted_iota(jnp.int32, (1, 128), 1)
    for t in range(2):
        row = jnp.full((1, 128), ZERO, jnp.int32)
        for slot in range(KCAP_L + KCAP_R):
            if slot < KCAP_L:
                tile, live = lad_ids[t, slot], slot < lad_n[t, 0]
            else:
                tile, live = cyc_ids[t, slot - KCAP_L] + KLT, slot - KCAP_L < cyc_n[t, 0]
            code = VAR * ((slot % 2 + tile) % 2) + slot // 2
            row = jnp.where(lane == jnp.where(live, tile, -1), code, row)
        tab_own[t] = row
    for h in range(2):
        tab_v[h, 0, c] = tab_own[c]

    pl.semaphore_wait(barrier, len(peers))

    def mates(side):
        return [
            to_mate(0, own.at[other, 0], held.at[0, 0, side]),
            to_mate(1, own.at[other, 1], held.at[1, 0, side]),
            to_mate(2, tab_own.at[other], tab_v.at[0, 0, side]),
            to_mate(3, tab_own.at[other], tab_v.at[1, 0, side]),
            to_mate(4, lad, panel.at[side, pl.ds(0, 1536)]),
            to_mate(5, cyc, panel.at[side, pl.ds(1536, 512)]),
        ]

    going = mates(c)
    coming = mates(other)
    for copy in going:
        copy.start()

    def hop(h, up, src, dst, kg, piece):
        rows = pl.ds(CUT * piece, CUT)
        return pltpu.make_async_remote_copy(
            src_ref=held.at[h, src, kg, rows], dst_ref=held.at[h, dst, kg, rows],
            send_sem=ring_s.at[h, dst, kg, piece], recv_sem=ring_r.at[h, dst, kg, piece],
            device_id=nxt[h] if up else prv[h], device_id_type=MESH)

    def tab_hop(h, up, src, dst):
        return pltpu.make_async_remote_copy(
            src_ref=tab_v.at[h, src], dst_ref=tab_v.at[h, dst],
            send_sem=tab_ss.at[h, dst], recv_sem=tab_rs.at[h, dst],
            device_id=nxt[h] if up else prv[h], device_id_type=MESH)

    def tab_down(h, slot):
        return pltpu.make_async_copy(tab_v.at[h, slot], tab_s.at[h, slot], tab_ls.at[h, slot])

    for copy in own_here:
        copy.wait()
    for piece in range(CUTS):
        for h in range(2):
            hop(h, True, 0, 1, c, piece).start()
            hop(h, False, 0, 31, c, piece).start()
    for h in range(2):
        coming[2 + h].wait_recv()
        tab_hop(h, True, 0, 1).start()
        tab_hop(h, False, 0, 31).start()
        tab_down(h, 0).start()
    for h in range(2):
        coming[h].wait_recv()
        for piece in range(CUTS):
            hop(h, True, 0, 1, other, piece).start()
            hop(h, False, 0, 31, other, piece).start()

    spread[ZERO] = jnp.zeros((HALF, 128), jnp.bfloat16)
    spread[VAR + ZERO] = jnp.zeros((HALF, 128), jnp.bfloat16)

    @pl.loop(0, 32)
    def _(i):
        tile = owners[16 * (i // 8) + 8 * c + i % 8]
        src = tile // 2
        for h in range(2):
            m = (pos[h] + 32 - POS[h](src // 4, src % 4)) % 32
            far = jnp.where(m >= STEPS, 1, 0)
            b = jnp.where(m >= STEPS, 31 - m, m)
            loc[2 * i + h] = (tile % 2 * STEPS + b) * 4 + 2 * h + far

    left = lax.broadcasted_iota(jnp.int32, (HALF, 128), 1) < 64

    def reduce_copy(b, r):
        to = (x + r) % 4
        return pltpu.make_async_remote_copy(
            src_ref=part.at[b, to], dst_ref=got.at[b, r - 1],
            send_sem=red_s.at[b, r - 1], recv_sem=red_r.at[b, r - 1],
            device_id=(2 * to + c, d), device_id_type=MESH)

    def share_copy(b, side):
        rows = total.at[pl.ds((side * STEPS + b) * 4, 4)]
        return pltpu.make_async_remote_copy(
            src_ref=rows, dst_ref=rows, send_sem=sh_s.at[b], recv_sem=sh_r.at[b],
            device_id=mate, device_id_type=MESH)

    def finish(b):
        for r in (1, 2, 3):
            reduce_copy(b, r).wait_recv()
        s = part[b, x] + got[b, 0] + got[b, 1] + got[b, 2]
        for q in range(4):
            total[(c * STEPS + b) * 4 + q] = s[HALF * q:HALF * (q + 1)]
        share_copy(b, c).start()

    def compute(b):
        for h in range(2):
            tab_down(h, b).wait()
            tab_down(h, 31 - b).wait()
        for kg in range(2):
            for q in range(4):
                h = q // 2
                m = b if q % 2 == 0 else 31 - b
                for p in range(PAIRS):
                    v = held[h, m, kg, p]
                    spread[p] = v
                    spread[VAR + p] = jnp.concatenate([v[:, 64:], v[:, :64]], axis=1)
                for j in range(16):
                    a = tab_s[h, m, kg, 0, 2 * j]
                    e = tab_s[h, m, kg, 0, 2 * j + 1]
                    lhs[HALF * q:HALF * (q + 1), 128 * j:128 * (j + 1)] = jnp.where(left, spread[a], spread[e])
            prod = jnp.dot(lhs[...], panel[kg], preferred_element_type=jnp.float32)
            for q in range(4):
                piece = prod[:, 128 * q:128 * (q + 1)]
                part[b, q] = piece if kg == 0 else part[b, q] + piece
        for r in (2, 1, 3):
            reduce_copy(b, r).start()

    @pl.loop(0, STEPS)
    def _(b):
        for h in range(2):
            @pl.when(b < 15)
            def _():
                tab_hop(h, True, b, b + 1).wait_recv()
                tab_down(h, b + 1).start()

            @pl.when(b < 14)
            def _():
                tab_hop(h, True, b + 1, b + 2).start()

            tab_hop(h, False, 0, 31 - b).wait_recv()
            tab_down(h, 31 - b).start()

            @pl.when(b < 15)
            def _():
                tab_hop(h, False, 31 - b, 30 - b).start()

        for kg in range(2):
            for piece in range(CUTS):
                up_end, down_end = (15, 14) if kg == 0 else (14, 15)
                for h in range(2):
                    @pl.when(b < 15)
                    def _():
                        hop(h, True, b, b + 1, kg, piece).wait_recv()

                    @pl.when(b < up_end)
                    def _():
                        hop(h, True, b + 1, b + 2, kg, piece).start()

                    hop(h, False, 0, 31 - b, kg, piece).wait_recv()

                    @pl.when(b < down_end)
                    def _():
                        hop(h, False, 31 - b, 30 - b, kg, piece).start()

        @pl.when(b == 2)
        def _():
            for copy in panels_here:
                copy.wait()
            for copy in coming[4:]:
                copy.wait_recv()

        first = jnp.where(b < 3, 0, jnp.where(b < 4, 2, b))
        last = jnp.where(b < 2, 0, jnp.where(b < 3, 2, b + 1))

        @pl.loop(first, last)
        def _(i):
            compute(i)

            @pl.when(i >= 2)
            def _():
                finish(i - 2)

    finish(STEPS - 2)
    finish(STEPS - 1)

    @pl.loop(0, STEPS)
    def _(b):
        share_copy(b, other).wait_recv()

    def final_copy(r):
        to = (x + r) % 4
        return pltpu.make_async_remote_copy(
            src_ref=fin_s.at[r], dst_ref=fin_r.at[r - 1], send_sem=fin_ss.at[r - 1], recv_sem=fin_rs.at[r - 1],
            device_id=(2 * to + c, d), device_id_type=MESH)

    for r in (2, 1, 3, 0):
        to = (x + r) % 4
        for i in range(16):
            fin_s[r, HALF * i:HALF * (i + 1)] = total[loc[to * 16 + i]]
        if r:
            final_copy(r).start()
    def columns(of):
        return pl.ds(pl.multiple_of(128 * of, 128), 128)

    out[:, columns(x)] = fin_s[0]
    for r in (1, 3, 2):
        final_copy(r).wait_recv()
        out[:, columns((x + 4 - r) % 4)] = fin_r[r - 1]

    for copy in going:
        copy.wait_send()
    for r in (1, 2, 3):
        final_copy(r).wait_send()

    @pl.loop(0, STEPS)
    def _(b):
        share_copy(b, c).wait_send()
        for r in (1, 2, 3):
            reduce_copy(b, r).wait_send()

    @pl.loop(1, 32)
    def _(m):
        for h in range(2):
            tab_hop(h, True, 0, m).wait_send()
            for kg in range(2):
                for piece in range(CUTS):
                    hop(h, True, 0, m, kg, piece).wait_send()


def per_device(
    ladder_amps, ladder_ids, ladder_count, cycle_amps, cycle_ids, cycle_count,
    ladder_panel, cycle_panel, owners, base,
):
    i32 = jnp.int32
    amps = jnp.concatenate([ladder_amps, cycle_amps], axis=1)
    own = amps.reshape(2, PAIRS, 2, 2, HALF, TS).transpose(0, 3, 1, 4, 2, 5).reshape(2, 2, PAIRS, HALF, 128)

    hbm = pl.BlockSpec(memory_space=pl.ANY)
    smem = pl.BlockSpec(memory_space=pltpu.SMEM)
    bf16, f32 = jnp.bfloat16, jnp.float32
    dma = pltpu.SemaphoreType.DMA
    summed = pl.pallas_call(
        kernel,
        name="ladder_ring",
        out_shape=jax.ShapeDtypeStruct((512, 512), f32),
        in_specs=[hbm] + [smem] * 5 + [hbm, hbm],
        out_specs=pl.BlockSpec(memory_space=pltpu.VMEM),
        scratch_shapes=[
            pltpu.VMEM((2, 32, 2, PAIRS, HALF, 128), bf16),
            pltpu.VMEM((2, 1, 128), i32),
            pltpu.VMEM((2, 32, 2, 1, 128), i32),
            pltpu.SMEM((2, 32, 2, 1, 128), i32),
            pltpu.SMEM((64,), i32),
            pltpu.VMEM((2, 2048, 512), bf16),
            pltpu.VMEM((2 * VAR, HALF, 128), bf16),
            pltpu.VMEM((128, 2048), bf16),
            pltpu.VMEM((STEPS, 4, 128, 128), f32),
            pltpu.VMEM((STEPS, 3, 128, 128), f32),
            pltpu.VMEM((2 * STEPS * 4, HALF, 128), f32),
            pltpu.VMEM((4, 512, 128), f32),
            pltpu.VMEM((3, 512, 128), f32),
            dma((4,)), dma((6,)), dma((6,)), dma((2, 32)), dma((2, 32)), dma((2, 32)),
            dma((2, 32, 2, CUTS)), dma((2, 32, 2, CUTS)),
            dma((STEPS, 3)), dma((STEPS, 3)), dma((STEPS,)), dma((STEPS,)),
            dma((3,)), dma((3,)),
        ],
        compiler_params=pltpu.CompilerParams(has_side_effects=True, collective_id=0, vmem_limit_bytes=58 * 2**20),
    )(own, ladder_ids, ladder_count, cycle_ids, cycle_count, owners, ladder_panel, cycle_panel)
    return base + summed


def solution(mesh):
    placed = (
        P("dev", "grp", None),
        P("dev", "grp"),
        P("dev", "grp"),
        P("dev", "grp", None),
        P("dev", "grp"),
        P("dev", "grp"),
        P("grp", "dev"),
        P("grp", "dev"),
        P(),
        P("grp", "dev"),
    )
    return jax.shard_map(
        per_device, mesh=mesh, in_specs=placed, out_specs=P("grp", "dev"), check_vma=False
    )
```

```python
import jax
import jax.numpy as jnp
from jax import lax
from jax.experimental import pallas as pl
from jax.experimental.pallas import tpu as pltpu
from jax.sharding import PartitionSpec as P

TS = 64
KLT = 24
KRT = 8
MESH = pl.DeviceIdType.MESH
STEPS = 16
HALF = 32
KCAP_L = 18
KCAP_R = 6
SLOTS = KCAP_L + KCAP_R
CUTS = 2
CUT = SLOTS // CUTS
ZERO = SLOTS
VAR = SLOTS + 1


def pos_first(z, y):
    return 4 * z + (y + z) % 4


def dev_first(s):
    k = s // 4
    return 4 * k + (s % 4 + 32 - k) % 4


def pos_second(z, y):
    t = (z + 24 - 3 * y) % 8
    return 4 * y + 16 * (t // 4) + t % 4


def dev_second(s):
    k = s // 4
    return 4 * ((3 * k + s % 4) % 8) + k % 4


POS = (pos_first, pos_second)
DEV = (dev_first, dev_second)


def kernel(
    lad_own, cyc_own, lad_ids, lad_n, cyc_ids, cyc_n, owners, lad, cyc, out,
    held, tab_own, tab_v, tab_s, loc, panel, spread, lhs, part, got, total, fin_s, fin_r,
    local_sem, pair_s, pair_r, tab_ss, tab_rs, tab_ls, ring_s, ring_r,
    red_s, red_r, sh_s, sh_r, fin_ss, fin_rs,
):
    g = lax.axis_index("grp")
    d = lax.axis_index("dev")
    x = g // 2
    c = g % 2
    z = d // 4
    y = d % 4
    other = 1 - c
    mate = (2 * x + other, d)
    across = [(x + r) % 4 for r in range(4)]
    pos = [POS[h](z, y) for h in range(2)]
    nxt = [(g, DEV[h]((pos[h] + 1) % 32)) for h in range(2)]
    prv = [(g, DEV[h]((pos[h] + 31) % 32)) for h in range(2)]

    def local(i, src, dst):
        return pltpu.make_async_copy(src, dst, local_sem.at[i])

    def to_mate(i, src, dst):
        return pltpu.make_async_remote_copy(
            src_ref=src, dst_ref=dst, send_sem=pair_s.at[i], recv_sem=pair_r.at[i],
            device_id=mate, device_id_type=MESH)

    def own_parts(h, tile, side):
        return [
            (lad_own.at[:, tile, h], held.at[h, 0, side, pl.ds(0, KCAP_L)]),
            (cyc_own.at[:, tile, h], held.at[h, 0, side, pl.ds(KCAP_L, KCAP_R)]),
        ]

    own_here = [local(2 * h + i, *own_parts(h, c, c)[i]) for h in range(2) for i in range(2)]
    panels_here = [
        local(4, lad, panel.at[c, pl.ds(0, 1536)]),
        local(5, cyc, panel.at[c, pl.ds(1536, 512)]),
    ]
    for copy in own_here + panels_here:
        copy.start()

    barrier = pltpu.get_barrier_semaphore()
    peers = nxt + prv + [mate] + [(2 * across[r] + c, d) for r in (1, 2, 3)]
    for p in peers:
        pl.semaphore_signal(barrier, inc=1, device_id=p, device_id_type=MESH)

    lane = lax.broadcasted_iota(jnp.int32, (1, 128), 1)
    for t in range(2):
        row = jnp.full((1, 128), ZERO, jnp.int32)
        for slot in range(KCAP_L + KCAP_R):
            if slot < KCAP_L:
                tile, live = lad_ids[t, slot], slot < lad_n[t]
            else:
                tile, live = cyc_ids[t, slot - KCAP_L] + KLT, slot - KCAP_L < cyc_n[t]
            row = jnp.where(lane == jnp.where(live, tile, -1), slot, row)
        tab_own[t] = row
    for h in range(2):
        tab_v[h, 0, c] = tab_own[c]

    pl.semaphore_wait(barrier, len(peers))

    def mates(side):
        return [
            to_mate(2 * h + i, *own_parts(h, other, side)[i]) for h in range(2) for i in range(2)
        ] + [
            to_mate(4, tab_own.at[other], tab_v.at[0, 0, side]),
            to_mate(5, tab_own.at[other], tab_v.at[1, 0, side]),
            to_mate(6, lad, panel.at[side, pl.ds(0, 1536)]),
            to_mate(7, cyc, panel.at[side, pl.ds(1536, 512)]),
        ]

    going = mates(c)
    coming = mates(other)
    for copy in going:
        copy.start()

    def hop(h, up, src, dst, kg, piece):
        rows = pl.ds(CUT * piece, CUT)
        return pltpu.make_async_remote_copy(
            src_ref=held.at[h, src, kg, rows], dst_ref=held.at[h, dst, kg, rows],
            send_sem=ring_s.at[h], recv_sem=ring_r.at[h, dst, kg, piece],
            device_id=nxt[h] if up else prv[h], device_id_type=MESH)

    def tab_hop(h, up, src, dst):
        return pltpu.make_async_remote_copy(
            src_ref=tab_v.at[h, src], dst_ref=tab_v.at[h, dst],
            send_sem=tab_ss.at[h], recv_sem=tab_rs.at[h, dst],
            device_id=nxt[h] if up else prv[h], device_id_type=MESH)

    def tab_down(h, slot):
        return pltpu.make_async_copy(tab_v.at[h, slot], tab_s.at[h, slot], tab_ls.at[h, slot])

    for copy in own_here:
        copy.wait()
    for piece in range(CUTS):
        for h in range(2):
            hop(h, True, 0, 1, c, piece).start()
            hop(h, False, 0, 31, c, piece).start()
    for h in range(2):
        coming[4 + h].wait_recv()
        tab_hop(h, True, 0, 1).start()
        tab_hop(h, False, 0, 31).start()
        tab_down(h, 0).start()
    for h in range(2):
        coming[2 * h].wait_recv()
        coming[2 * h + 1].wait_recv()
        for piece in range(CUTS):
            hop(h, True, 0, 1, other, piece).start()
            hop(h, False, 0, 31, other, piece).start()

    spread[ZERO] = jnp.zeros((16, 128), jnp.bfloat16)
    spread[VAR + ZERO] = jnp.zeros((16, 128), jnp.bfloat16)

    def seat(h, row, col):
        if h == 0:
            return 4 * row + ((col + row) & 3)
        t = (row + 24 - 3 * col) & 7
        return 4 * col + 16 * (t >> 2) + (t & 3)

    @pl.loop(0, 4)
    def _(to):
        for i in range(8):
            tile = owners[16 * to + 8 * c + i]
            row, col = tile >> 3, (tile >> 1) & 3
            for h in range(2):
                m = (pos[h] + 32 - seat(h, row, col)) & 31
                near = m < STEPS
                b = jnp.where(near, m, 31 - m)
                q = jnp.where(near, 2 * h, 2 * h + 1)
                loc[16 * to + 2 * i + h] = 4 * (STEPS * (tile & 1) + b) + q

    left = lax.broadcasted_iota(jnp.int32, (16, 128), 1) < 64

    def reduce_copy(b, r):
        to = across[r]
        return pltpu.make_async_remote_copy(
            src_ref=part.at[b, to], dst_ref=got.at[b, r - 1],
            send_sem=red_s, recv_sem=red_r.at[b, r - 1],
            device_id=(2 * to + c, d), device_id_type=MESH)

    def share_copy(b, side):
        rows = total.at[pl.ds((side * STEPS + b) * 4, 4)]
        return pltpu.make_async_remote_copy(
            src_ref=rows, dst_ref=rows, send_sem=sh_s, recv_sem=sh_r.at[b],
            device_id=mate, device_id_type=MESH)

    def finish(b):
        for r in (1, 2, 3):
            reduce_copy(b, r).wait_recv()
        s = part[b, x] + got[b, 0] + got[b, 1] + got[b, 2]
        for q in range(4):
            total[(c * STEPS + b) * 4 + q] = s[HALF * q:HALF * (q + 1)]
        share_copy(b, c).start()

    def compute(b):
        for h in range(2):
            tab_down(h, b).wait()
            tab_down(h, 31 - b).wait()
        for kg in range(2):
            for q in range(4):
                h = q // 2
                m = b if q % 2 == 0 else 31 - b
                for p in range(SLOTS):
                    v = held[h, m, kg, p]
                    spread[p] = v
                    spread[VAR + p] = jnp.concatenate([v[:, 64:], v[:, :64]], axis=1)
                for j in range(16):
                    a = tab_s[h, m, kg, 0, 2 * j]
                    e = tab_s[h, m, kg, 0, 2 * j + 1]
                    at = slice(128 * j, 128 * (j + 1))
                    lhs[HALF * q:HALF * q + 16, at] = jnp.where(left, spread[a], spread[VAR + e])
                    lhs[HALF * q + 16:HALF * (q + 1), at] = jnp.where(left, spread[VAR + a], spread[e])
            prod = jnp.dot(lhs[...], panel[kg], preferred_element_type=jnp.float32)
            for q in range(4):
                piece = prod[:, 128 * q:128 * (q + 1)]
                part[b, q] = piece if kg == 0 else part[b, q] + piece
        for r in (2, 1, 3):
            reduce_copy(b, r).start()

    @pl.loop(0, STEPS)
    def _(b):
        for h in range(2):
            @pl.when(b < 15)
            def _():
                tab_hop(h, True, b, b + 1).wait_recv()
                tab_down(h, b + 1).start()

            @pl.when(b < 14)
            def _():
                tab_hop(h, True, b + 1, b + 2).start()

            tab_hop(h, False, 0, 31 - b).wait_recv()
            tab_down(h, 31 - b).start()

            @pl.when(b < 15)
            def _():
                tab_hop(h, False, 31 - b, 30 - b).start()

        for kg in range(2):
            for piece in range(CUTS):
                up_end, down_end = (15, 14) if kg == 0 else (14, 15)
                for h in range(2):
                    @pl.when(b < 15)
                    def _():
                        hop(h, True, b, b + 1, kg, piece).wait_recv()

                    @pl.when(b < up_end)
                    def _():
                        hop(h, True, b + 1, b + 2, kg, piece).start()

                    hop(h, False, 0, 31 - b, kg, piece).wait_recv()

                    @pl.when(b < down_end)
                    def _():
                        hop(h, False, 31 - b, 30 - b, kg, piece).start()

        @pl.when(b == 2)
        def _():
            for copy in panels_here:
                copy.wait()
            for copy in coming[6:]:
                copy.wait_recv()

        first = jnp.where(b < 3, 0, jnp.where(b < 4, 2, b))
        last = jnp.where(b < 2, 0, jnp.where(b < 3, 2, b + 1))

        @pl.loop(first, last)
        def _(i):
            compute(i)

            @pl.when(i >= 2)
            def _():
                finish(i - 2)

    finish(STEPS - 2)
    finish(STEPS - 1)

    @pl.loop(0, STEPS)
    def _(b):
        share_copy(b, other).wait_recv()

    def final_copy(r):
        to = across[r]
        return pltpu.make_async_remote_copy(
            src_ref=fin_s.at[r], dst_ref=fin_r.at[r - 1], send_sem=fin_ss, recv_sem=fin_rs.at[r - 1],
            device_id=(2 * to + c, d), device_id_type=MESH)

    for r in (2, 1, 3, 0):
        to = across[r]
        for i in range(16):
            rows = total[loc[to * 16 + i]]
            fin_s[r, pl.ds(HALF * i, 16, stride=2)] = rows[:16]
            fin_s[r, pl.ds(HALF * i + 1, 16, stride=2)] = rows[16:]
        if r:
            final_copy(r).start()
    def columns(of):
        return pl.ds(pl.multiple_of(128 * of, 128), 128)

    out[:, columns(x)] = fin_s[0]

    def drain(ref, sem):
        pltpu.make_async_copy(ref, ref, sem).wait()

    for copy in going:
        copy.wait_send()
    for h in range(2):
        drain(held.at[h, pl.ds(0, 31)], ring_s.at[h])
        drain(tab_v.at[h, pl.ds(0, 31)], tab_ss.at[h])
    drain(got, red_s)
    drain(total.at[pl.ds(0, 4 * STEPS)], sh_s)

    for r in (1, 3, 2):
        final_copy(r).wait_recv()
        out[:, columns(across[4 - r])] = fin_r[r - 1]
    drain(fin_r, fin_ss)


def per_device(
    ladder_amps, ladder_ids, ladder_count, cycle_amps, cycle_ids, cycle_count,
    ladder_panel, cycle_panel, owners, base,
):
    i32 = jnp.int32
    lad_own = ladder_amps.transpose(1, 0, 2).reshape(KCAP_L, 2, 2, 16, 128)
    cyc_own = cycle_amps.transpose(1, 0, 2).reshape(KCAP_R, 2, 2, 16, 128)
    lad_n, cyc_n = ladder_count.reshape(2), cycle_count.reshape(2)

    hbm = pl.BlockSpec(memory_space=pl.ANY)
    smem = pl.BlockSpec(memory_space=pltpu.SMEM)
    bf16, f32 = jnp.bfloat16, jnp.float32
    dma = pltpu.SemaphoreType.DMA
    summed = pl.pallas_call(
        kernel,
        name="ladder_ring",
        out_shape=jax.ShapeDtypeStruct((512, 512), f32),
        in_specs=[hbm] * 2 + [smem] * 5 + [hbm, hbm],
        out_specs=pl.BlockSpec(memory_space=pltpu.VMEM),
        scratch_shapes=[
            pltpu.VMEM((2, 32, 2, SLOTS, 16, 128), bf16),
            pltpu.VMEM((2, 1, 128), i32),
            pltpu.VMEM((2, 32, 2, 1, 128), i32),
            pltpu.SMEM((2, 32, 2, 1, 128), i32),
            pltpu.SMEM((64,), i32),
            pltpu.VMEM((2, 2048, 512), bf16),
            pltpu.VMEM((2 * VAR, 16, 128), bf16),
            pltpu.VMEM((128, 2048), bf16),
            pltpu.VMEM((STEPS, 4, 128, 128), f32),
            pltpu.VMEM((STEPS, 3, 128, 128), f32),
            pltpu.VMEM((2 * STEPS * 4, HALF, 128), f32),
            pltpu.VMEM((4, 512, 128), f32),
            pltpu.VMEM((3, 512, 128), f32),
            dma((6,)), dma((8,)), dma((8,)), dma((2,)), dma((2, 32)), dma((2, 32)),
            dma((2,)), dma((2, 32, 2, CUTS)),
            dma, dma((STEPS, 3)), dma, dma((STEPS,)), dma, dma((3,)),
        ],
        compiler_params=pltpu.CompilerParams(has_side_effects=True, collective_id=0, vmem_limit_bytes=58 * 2**20),
    )(lad_own, cyc_own, ladder_ids, lad_n, cycle_ids, cyc_n, owners, ladder_panel, cycle_panel)
    return base + summed


def solution(mesh):
    placed = (
        P("dev", "grp", None),
        P("dev", "grp"),
        P("dev", "grp"),
        P("dev", "grp", None),
        P("dev", "grp"),
        P("dev", "grp"),
        P("grp", "dev"),
        P("grp", "dev"),
        P(),
        P("grp", "dev"),
    )
    return jax.shard_map(
        per_device, mesh=mesh, in_specs=placed, out_specs=P("grp", "dev"), check_vma=False
    )
```

```python
import jax
import jax.numpy as jnp
from jax import lax
from jax.experimental import pallas as pl
from jax.experimental.pallas import tpu as pltpu
from jax.sharding import PartitionSpec as P

TS = 64
KLT = 24
KRT = 8
MESH = pl.DeviceIdType.MESH
STEPS = 16
HALF = 32
KCAP_L = 18
KCAP_R = 6
SLOTS = KCAP_L + KCAP_R
CUTS = 2
CUT = SLOTS // CUTS
ZERO = SLOTS
VAR = SLOTS + 1


def pos_first(z, y):
    return 4 * z + (y + z) % 4


def dev_first(s):
    k = s // 4
    return 4 * k + (s % 4 + 32 - k) % 4


def pos_second(z, y):
    t = (z + 24 - 3 * y) % 8
    return 4 * y + 16 * (t // 4) + t % 4


def dev_second(s):
    k = s // 4
    return 4 * ((3 * k + s % 4) % 8) + k % 4


POS = (pos_first, pos_second)
DEV = (dev_first, dev_second)


def kernel(
    lad_amps, cyc_amps, lad_ids, lad_n, cyc_ids, cyc_n, owners, lad, cyc, base, out,
    amps_l, amps_c, own, held, tab_own, tab_v, tab_s, loc, panel, spread, lhs, part, got, total, fin_s, fin_r, base_v,
    local_sem, pair_s, pair_r, tab_ss, tab_rs, tab_ls, ring_s, ring_r,
    red_s, red_r, sh_s, sh_r, fin_ss, fin_rs,
):
    g = lax.axis_index("grp")
    d = lax.axis_index("dev")
    x = g // 2
    c = g % 2
    z = d // 4
    y = d % 4
    other = 1 - c
    mate = (2 * x + other, d)
    across = [(x + r) % 4 for r in range(4)]
    pos = [POS[h](z, y) for h in range(2)]
    nxt = [(g, DEV[h]((pos[h] + 1) % 32)) for h in range(2)]
    prv = [(g, DEV[h]((pos[h] + 31) % 32)) for h in range(2)]

    def local(i, src, dst):
        return pltpu.make_async_copy(src, dst, local_sem.at[i])

    def to_mate(i, src, dst):
        return pltpu.make_async_remote_copy(
            src_ref=src, dst_ref=dst, send_sem=pair_s.at[i], recv_sem=pair_r.at[i],
            device_id=mate, device_id_type=MESH)

    amps_here = [local(0, lad_amps, amps_l), local(1, cyc_amps, amps_c)]
    panels_here = [
        local(2, lad, panel.at[c, pl.ds(0, 1536)]),
        local(3, cyc, panel.at[c, pl.ds(1536, 512)]),
    ]
    base_here = local(4, base, base_v)
    for copy in amps_here + panels_here + [base_here]:
        copy.start()

    barrier = pltpu.get_barrier_semaphore()
    peers = nxt + prv + [mate] + [(2 * across[r] + c, d) for r in (1, 2, 3)]
    for p in peers:
        pl.semaphore_signal(barrier, inc=1, device_id=p, device_id_type=MESH)

    lane = lax.broadcasted_iota(jnp.int32, (1, 128), 1)
    for t in range(2):
        row = jnp.full((1, 128), ZERO, jnp.int32)
        for slot in range(KCAP_L + KCAP_R):
            if slot < KCAP_L:
                tile, live = lad_ids[t, slot], slot < lad_n[t]
            else:
                tile, live = cyc_ids[t, slot - KCAP_L] + KLT, slot - KCAP_L < cyc_n[t]
            row = jnp.where(lane == jnp.where(live, tile, -1), slot, row)
        tab_own[t] = row
    for copy in amps_here:
        copy.wait()
    for t in range(2):
        for amps, first, count in ((amps_l, 0, KCAP_L), (amps_c, KCAP_L, KCAP_R)):
            pairs = amps[:, t, :].reshape(count, HALF, 128)
            for h in range(2):
                own[t, h, first:first + count] = pairs[:, 16 * h:16 * (h + 1)]
    for h in range(2):
        held[h, 0, c] = own[c, h]
        tab_v[h, 0, c] = tab_own[c]

    pl.semaphore_wait(barrier, len(peers))

    def mates(side):
        return [
            to_mate(0, own.at[other, 0], held.at[0, 0, side]),
            to_mate(1, own.at[other, 1], held.at[1, 0, side]),
            to_mate(2, tab_own.at[other], tab_v.at[0, 0, side]),
            to_mate(3, tab_own.at[other], tab_v.at[1, 0, side]),
            to_mate(4, lad, panel.at[side, pl.ds(0, 1536)]),
            to_mate(5, cyc, panel.at[side, pl.ds(1536, 512)]),
        ]

    going = mates(c)
    coming = mates(other)
    for copy in going:
        copy.start()

    def hop(h, up, src, dst, kg, piece):
        rows = pl.ds(CUT * piece, CUT)
        return pltpu.make_async_remote_copy(
            src_ref=held.at[h, src, kg, rows], dst_ref=held.at[h, dst, kg, rows],
            send_sem=ring_s.at[h], recv_sem=ring_r.at[h, dst, kg, piece],
            device_id=nxt[h] if up else prv[h], device_id_type=MESH)

    def tab_hop(h, up, src, dst):
        return pltpu.make_async_remote_copy(
            src_ref=tab_v.at[h, src], dst_ref=tab_v.at[h, dst],
            send_sem=tab_ss.at[h], recv_sem=tab_rs.at[h, dst],
            device_id=nxt[h] if up else prv[h], device_id_type=MESH)

    def tab_down(h, slot):
        return pltpu.make_async_copy(tab_v.at[h, slot], tab_s.at[h, slot], tab_ls.at[h, slot])

    for piece in range(CUTS):
        for h in range(2):
            hop(h, True, 0, 1, c, piece).start()
            hop(h, False, 0, 31, c, piece).start()
    for h in range(2):
        coming[2 + h].wait_recv()
        tab_hop(h, True, 0, 1).start()
        tab_hop(h, False, 0, 31).start()
        tab_down(h, 0).start()
    for h in range(2):
        coming[h].wait_recv()
        for piece in range(CUTS):
            hop(h, True, 0, 1, other, piece).start()
            hop(h, False, 0, 31, other, piece).start()

    spread[ZERO] = jnp.zeros((16, 128), jnp.bfloat16)
    spread[VAR + ZERO] = jnp.zeros((16, 128), jnp.bfloat16)

    def seat(h, row, col):
        if h == 0:
            return 4 * row + ((col + row) & 3)
        t = (row + 24 - 3 * col) & 7
        return 4 * col + 16 * (t >> 2) + (t & 3)

    @pl.loop(0, 4)
    def _(to):
        for i in range(8):
            tile = owners[16 * to + 8 * c + i]
            row, col = tile >> 3, (tile >> 1) & 3
            for h in range(2):
                m = (pos[h] + 32 - seat(h, row, col)) & 31
                near = m < STEPS
                b = jnp.where(near, m, 31 - m)
                q = jnp.where(near, 2 * h, 2 * h + 1)
                loc[16 * to + 2 * i + h] = 4 * (STEPS * (tile & 1) + b) + q

    left = lax.broadcasted_iota(jnp.int32, (16, 128), 1) < 64

    def reduce_copy(b, r):
        to = across[r]
        return pltpu.make_async_remote_copy(
            src_ref=part.at[b, to], dst_ref=got.at[b, r - 1],
            send_sem=red_s, recv_sem=red_r.at[b, r - 1],
            device_id=(2 * to + c, d), device_id_type=MESH)

    def share_copy(b, side):
        rows = total.at[pl.ds((side * STEPS + b) * 4, 4)]
        return pltpu.make_async_remote_copy(
            src_ref=rows, dst_ref=rows, send_sem=sh_s, recv_sem=sh_r.at[b],
            device_id=mate, device_id_type=MESH)

    def finish(b):
        for r in (1, 2, 3):
            reduce_copy(b, r).wait_recv()
        s = part[b, x] + got[b, 0] + got[b, 1] + got[b, 2]
        for q in range(4):
            total[(c * STEPS + b) * 4 + q] = s[HALF * q:HALF * (q + 1)]
        share_copy(b, c).start()

    def compute(b, kg):
        for q in range(4):
            h = q // 2
            m = b if q % 2 == 0 else 31 - b
            for p in range(SLOTS):
                v = held[h, m, kg, p]
                spread[p] = v
                spread[VAR + p] = jnp.concatenate([v[:, 64:], v[:, :64]], axis=1)
            for j in range(16):
                a = tab_s[h, m, kg, 0, 2 * j]
                e = tab_s[h, m, kg, 0, 2 * j + 1]
                at = slice(128 * j, 128 * (j + 1))
                lhs[HALF * q:HALF * q + 16, at] = jnp.where(left, spread[a], spread[VAR + e])
                lhs[HALF * q + 16:HALF * (q + 1), at] = jnp.where(left, spread[VAR + a], spread[e])
        prod = jnp.dot(lhs[...], panel[kg], preferred_element_type=jnp.float32)
        for q in range(4):
            piece = prod[:, 128 * q:128 * (q + 1)]
            part[b, q] = piece if kg == 0 else part[b, q] + piece

    @pl.loop(0, STEPS)
    def _(b):
        for h in range(2):
            @pl.when(b < 15)
            def _():
                tab_hop(h, True, b, b + 1).wait_recv()
                tab_down(h, b + 1).start()

            @pl.when(b < 14)
            def _():
                tab_hop(h, True, b + 1, b + 2).start()

            tab_hop(h, False, 0, 31 - b).wait_recv()
            tab_down(h, 31 - b).start()

            @pl.when(b < 15)
            def _():
                tab_hop(h, False, 31 - b, 30 - b).start()

        @pl.when(b == 2)
        def _():
            for copy in panels_here:
                copy.wait()
            for copy in coming[4:]:
                copy.wait_recv()

        first = jnp.where(b < 3, 0, jnp.where(b < 4, 2, b))
        last = jnp.where(b < 2, 0, jnp.where(b < 3, 2, b + 1))

        for kg in range(2):
            for piece in range(CUTS):
                up_end, down_end = (15, 14) if kg == 0 else (14, 15)
                for h in range(2):
                    @pl.when(b < 15)
                    def _():
                        hop(h, True, b, b + 1, kg, piece).wait_recv()

                    @pl.when(b < up_end)
                    def _():
                        hop(h, True, b + 1, b + 2, kg, piece).start()

                    hop(h, False, 0, 31 - b, kg, piece).wait_recv()

                    @pl.when(b < down_end)
                    def _():
                        hop(h, False, 31 - b, 30 - b, kg, piece).start()

            @pl.loop(first, last)
            def _(i):
                if kg == 0:
                    for h in range(2):
                        tab_down(h, i).wait()
                        tab_down(h, 31 - i).wait()
                compute(i, kg)
                if kg == 0:
                    @pl.when(i >= 4)
                    def _():
                        finish(i - 4)
                else:
                    for r in (2, 1, 3):
                        reduce_copy(i, r).start()

    @pl.loop(STEPS - 4, STEPS)
    def _(b):
        finish(b)

    @pl.loop(0, STEPS)
    def _(b):
        share_copy(b, other).wait_recv()

    def final_copy(r):
        to = across[r]
        return pltpu.make_async_remote_copy(
            src_ref=fin_s.at[r], dst_ref=fin_r.at[r - 1], send_sem=fin_ss, recv_sem=fin_rs.at[r - 1],
            device_id=(2 * to + c, d), device_id_type=MESH)

    for r in (2, 1, 3, 0):
        to = across[r]
        for i in range(16):
            rows = total[loc[to * 16 + i]]
            fin_s[r, pl.ds(HALF * i, 16, stride=2)] = rows[:16]
            fin_s[r, pl.ds(HALF * i + 1, 16, stride=2)] = rows[16:]
        if r:
            final_copy(r).start()
    def columns(of):
        return pl.ds(pl.multiple_of(128 * of, 128), 128)

    base_here.wait()
    out[:, columns(x)] = base_v[:, columns(x)] + fin_s[0]

    def drain(ref, sem):
        pltpu.make_async_copy(ref, ref, sem).wait()

    for copy in going:
        copy.wait_send()
    for h in range(2):
        drain(held.at[h, pl.ds(0, 31)], ring_s.at[h])
        drain(tab_v.at[h, pl.ds(0, 31)], tab_ss.at[h])
    drain(got, red_s)
    drain(total.at[pl.ds(0, 4 * STEPS)], sh_s)

    for r in (1, 3, 2):
        final_copy(r).wait_recv()
        cols = columns(across[4 - r])
        out[:, cols] = base_v[:, cols] + fin_r[r - 1]
    drain(fin_r, fin_ss)


def per_device(
    ladder_amps, ladder_ids, ladder_count, cycle_amps, cycle_ids, cycle_count,
    ladder_panel, cycle_panel, owners, base,
):
    i32 = jnp.int32
    lad_amps, cyc_amps = ladder_amps.transpose(1, 0, 2), cycle_amps.transpose(1, 0, 2)
    lad_n, cyc_n = ladder_count.reshape(2), cycle_count.reshape(2)

    hbm = pl.BlockSpec(memory_space=pl.ANY)
    smem = pl.BlockSpec(memory_space=pltpu.SMEM)
    bf16, f32 = jnp.bfloat16, jnp.float32
    dma = pltpu.SemaphoreType.DMA
    summed = pl.pallas_call(
        kernel,
        name="ladder_ring",
        out_shape=jax.ShapeDtypeStruct((512, 512), f32),
        in_specs=[hbm] * 2 + [smem] * 5 + [hbm] * 3,
        out_specs=pl.BlockSpec(memory_space=pltpu.VMEM),
        scratch_shapes=[
            pltpu.VMEM((KCAP_L, 2, TS * TS), bf16),
            pltpu.VMEM((KCAP_R, 2, TS * TS), bf16),
            pltpu.VMEM((2, 2, SLOTS, 16, 128), bf16),
            pltpu.VMEM((2, 32, 2, SLOTS, 16, 128), bf16),
            pltpu.VMEM((2, 1, 128), i32),
            pltpu.VMEM((2, 32, 2, 1, 128), i32),
            pltpu.SMEM((2, 32, 2, 1, 128), i32),
            pltpu.SMEM((64,), i32),
            pltpu.VMEM((2, 2048, 512), bf16),
            pltpu.VMEM((2 * VAR, 16, 128), bf16),
            pltpu.VMEM((128, 2048), bf16),
            pltpu.VMEM((STEPS, 4, 128, 128), f32),
            pltpu.VMEM((STEPS, 3, 128, 128), f32),
            pltpu.VMEM((2 * STEPS * 4, HALF, 128), f32),
            pltpu.VMEM((4, 512, 128), f32),
            pltpu.VMEM((3, 512, 128), f32),
            pltpu.VMEM((512, 512), f32),
            dma((5,)), dma((6,)), dma((6,)), dma((2,)), dma((2, 32)), dma((2, 32)),
            dma((2,)), dma((2, 32, 2, CUTS)),
            dma, dma((STEPS, 3)), dma, dma((STEPS,)), dma, dma((3,)),
        ],
        compiler_params=pltpu.CompilerParams(has_side_effects=True, collective_id=0, vmem_limit_bytes=58 * 2**20),
    )(lad_amps, cyc_amps, ladder_ids, lad_n, cycle_ids, cyc_n, owners, ladder_panel, cycle_panel, base)
    return summed


def solution(mesh):
    placed = (
        P("dev", "grp", None),
        P("dev", "grp"),
        P("dev", "grp"),
        P("dev", "grp", None),
        P("dev", "grp"),
        P("dev", "grp"),
        P("grp", "dev"),
        P("grp", "dev"),
        P(),
        P("grp", "dev"),
    )
    return jax.shard_map(
        per_device, mesh=mesh, in_specs=placed, out_specs=P("grp", "dev"), check_vma=False
    )
```

```python
import jax
import jax.numpy as jnp
from jax import lax
from jax.experimental import pallas as pl
from jax.experimental.pallas import tpu as pltpu
from jax.sharding import PartitionSpec as P

TS = 64
KLT = 24
KRT = 8
MESH = pl.DeviceIdType.MESH
STEPS = 16
HALF = 32
KCAP_L = 18
KCAP_R = 6
SLOTS = KCAP_L + KCAP_R
CUTS = 2
CUT = SLOTS // CUTS
ZERO = SLOTS
VAR = SLOTS + 1


def pos_first(z, y):
    return 4 * z + (y + z) % 4


def dev_first(s):
    k = s // 4
    return 4 * k + (s % 4 + 32 - k) % 4


def pos_second(z, y):
    t = (z + 24 - 3 * y) % 8
    return 4 * y + 16 * (t // 4) + t % 4


def dev_second(s):
    k = s // 4
    return 4 * ((3 * k + s % 4) % 8) + k % 4


POS = (pos_first, pos_second)
DEV = (dev_first, dev_second)


def kernel(
    lad_amps, cyc_amps, lad_ids_h, lad_n_h, cyc_ids_h, cyc_n_h, owners_h, lad, cyc, base, out,
    lad_ids, lad_n, cyc_ids, cyc_n, owners,
    amps_l, amps_c, own, held, tab_own, tab_v, tab_s, loc, panel, spread, lhs, part, got, total, fin_s, fin_r, base_v,
    local_sem, pair_s, pair_r, tab_ss, tab_rs, tab_ls, ring_s, ring_r,
    red_s, red_r, sh_s, sh_r, fin_ss, fin_rs,
):
    g = lax.axis_index("grp")
    d = lax.axis_index("dev")
    x = g // 2
    c = g % 2
    z = d // 4
    y = d % 4
    other = 1 - c
    mate = (2 * x + other, d)
    across = [(x + r) % 4 for r in range(4)]
    pos = [POS[h](z, y) for h in range(2)]
    nxt = [(g, DEV[h]((pos[h] + 1) % 32)) for h in range(2)]
    prv = [(g, DEV[h]((pos[h] + 31) % 32)) for h in range(2)]

    def local(i, src, dst):
        return pltpu.make_async_copy(src, dst, local_sem.at[i])

    def to_mate(i, src, dst):
        return pltpu.make_async_remote_copy(
            src_ref=src, dst_ref=dst, send_sem=pair_s.at[i], recv_sem=pair_r.at[i],
            device_id=mate, device_id_type=MESH)

    barrier = pltpu.get_barrier_semaphore()
    peers = nxt + prv + [mate] + [(2 * across[r] + c, d) for r in (1, 2, 3)]
    for p in peers:
        pl.semaphore_signal(barrier, inc=1, device_id=p, device_id_type=MESH)

    amps_here = [local(0, lad_amps, amps_l), local(1, cyc_amps, amps_c)]
    panels_here = [
        local(2, lad, panel.at[c, pl.ds(0, 1536)]),
        local(3, cyc, panel.at[c, pl.ds(1536, 512)]),
    ]
    base_here = local(4, base, base_v)
    lists_here = [
        local(5, lad_ids_h, lad_ids), local(6, lad_n_h, lad_n),
        local(7, cyc_ids_h, cyc_ids), local(8, cyc_n_h, cyc_n), local(9, owners_h, owners),
    ]
    for copy in amps_here + lists_here + panels_here + [base_here]:
        copy.start()
    for copy in lists_here:
        copy.wait()

    lane = lax.broadcasted_iota(jnp.int32, (1, 128), 1)
    for t in range(2):
        row = jnp.full((1, 128), ZERO, jnp.int32)
        for slot in range(KCAP_L + KCAP_R):
            if slot < KCAP_L:
                tile, live = lad_ids[t, slot], slot < lad_n[t]
            else:
                tile, live = cyc_ids[t, slot - KCAP_L] + KLT, slot - KCAP_L < cyc_n[t]
            row = jnp.where(lane == jnp.where(live, tile, -1), slot, row)
        tab_own[t] = row
    for copy in amps_here:
        copy.wait()
    for t in range(2):
        for amps, first, count in ((amps_l, 0, KCAP_L), (amps_c, KCAP_L, KCAP_R)):
            pairs = amps[:, t, :].reshape(count, HALF, 128)
            for h in range(2):
                own[t, h, first:first + count] = pairs[:, 16 * h:16 * (h + 1)]
    for h in range(2):
        held[h, 0, c] = own[c, h]
        tab_v[h, 0, c] = tab_own[c]

    pl.semaphore_wait(barrier, len(peers))

    def mates(side):
        return [
            to_mate(0, own.at[other, 0], held.at[0, 0, side]),
            to_mate(1, own.at[other, 1], held.at[1, 0, side]),
            to_mate(2, tab_own.at[other], tab_v.at[0, 0, side]),
            to_mate(3, tab_own.at[other], tab_v.at[1, 0, side]),
            to_mate(4, lad, panel.at[side, pl.ds(0, 1536)]),
            to_mate(5, cyc, panel.at[side, pl.ds(1536, 512)]),
        ]

    going = mates(c)
    coming = mates(other)
    for copy in going:
        copy.start()

    def hop(h, up, src, dst, kg, piece):
        rows = pl.ds(CUT * piece, CUT)
        return pltpu.make_async_remote_copy(
            src_ref=held.at[h, src, kg, rows], dst_ref=held.at[h, dst, kg, rows],
            send_sem=ring_s.at[h], recv_sem=ring_r.at[h, dst, kg, piece],
            device_id=nxt[h] if up else prv[h], device_id_type=MESH)

    def tab_hop(h, up, src, dst):
        return pltpu.make_async_remote_copy(
            src_ref=tab_v.at[h, src], dst_ref=tab_v.at[h, dst],
            send_sem=tab_ss.at[h], recv_sem=tab_rs.at[h, dst],
            device_id=nxt[h] if up else prv[h], device_id_type=MESH)

    def tab_down(h, slot):
        return pltpu.make_async_copy(tab_v.at[h, slot], tab_s.at[h, slot], tab_ls.at[h, slot])

    for piece in range(CUTS):
        for h in range(2):
            hop(h, True, 0, 1, c, piece).start()
            hop(h, False, 0, 31, c, piece).start()
    for h in range(2):
        coming[2 + h].wait_recv()
        tab_hop(h, True, 0, 1).start()
        tab_hop(h, False, 0, 31).start()
        tab_down(h, 0).start()
    for h in range(2):
        coming[h].wait_recv()
        for piece in range(CUTS):
            hop(h, True, 0, 1, other, piece).start()
            hop(h, False, 0, 31, other, piece).start()

    spread[ZERO] = jnp.zeros((16, 128), jnp.bfloat16)
    spread[VAR + ZERO] = jnp.zeros((16, 128), jnp.bfloat16)

    def seat(h, row, col):
        if h == 0:
            return 4 * row + ((col + row) & 3)
        t = (row + 24 - 3 * col) & 7
        return 4 * col + 16 * (t >> 2) + (t & 3)

    @pl.loop(0, 4)
    def _(to):
        for i in range(8):
            tile = owners[16 * to + 8 * c + i]
            row, col = tile >> 3, (tile >> 1) & 3
            for h in range(2):
                m = (pos[h] + 32 - seat(h, row, col)) & 31
                near = m < STEPS
                b = jnp.where(near, m, 31 - m)
                q = jnp.where(near, h, 2 + h)
                loc[16 * to + 2 * i + h] = 4 * (STEPS * (tile & 1) + b) + q

    left = lax.broadcasted_iota(jnp.int32, (16, 128), 1) < 64

    def reduce_copy(b, r):
        to = across[r]
        return pltpu.make_async_remote_copy(
            src_ref=part.at[b, to], dst_ref=got.at[b, r - 1],
            send_sem=red_s, recv_sem=red_r.at[b, r - 1],
            device_id=(2 * to + c, d), device_id_type=MESH)

    def half_copy(b, r, half):
        to = across[r]
        rows = pl.ds(64 * half, 64)
        return pltpu.make_async_remote_copy(
            src_ref=part.at[b, to, rows], dst_ref=got.at[b, r - 1, rows],
            send_sem=red_s, recv_sem=red_r.at[b, r - 1],
            device_id=(2 * to + c, d), device_id_type=MESH)

    def share_copy(b, side):
        rows = total.at[pl.ds((side * STEPS + b) * 4, 4)]
        return pltpu.make_async_remote_copy(
            src_ref=rows, dst_ref=rows, send_sem=sh_s, recv_sem=sh_r.at[b],
            device_id=mate, device_id_type=MESH)

    def finish(b):
        for r in (1, 2, 3):
            reduce_copy(b, r).wait_recv()
        s = part[b, x] + got[b, 0] + got[b, 1] + got[b, 2]
        for q in range(4):
            total[(c * STEPS + b) * 4 + q] = s[HALF * q:HALF * (q + 1)]
        share_copy(b, c).start()

    def compute(b, kg, first, count):
        for n in range(count):
            q = first + n
            h = q % 2
            m = b if q < 2 else 31 - b
            for p in range(SLOTS):
                v = held[h, m, kg, p]
                spread[p] = v
                spread[VAR + p] = jnp.concatenate([v[:, 64:], v[:, :64]], axis=1)
            for j in range(16):
                a = tab_s[h, m, kg, 0, 2 * j]
                e = tab_s[h, m, kg, 0, 2 * j + 1]
                at = slice(128 * j, 128 * (j + 1))
                lhs[HALF * n:HALF * n + 16, at] = jnp.where(left, spread[a], spread[VAR + e])
                lhs[HALF * n + 16:HALF * (n + 1), at] = jnp.where(left, spread[VAR + a], spread[e])
        prod = jnp.dot(lhs[:HALF * count], panel[kg], preferred_element_type=jnp.float32)
        at = slice(HALF * first, HALF * (first + count))
        for q in range(4):
            piece = prod[:, 128 * q:128 * (q + 1)]
            part[b, q, at] = piece if kg == 0 else part[b, q, at] + piece

    @pl.loop(0, STEPS - 1)
    def _(b):
        for h in range(2):
            tab_hop(h, True, b, b + 1).wait_recv()
            tab_down(h, b + 1).start()

            @pl.when(b < 14)
            def _():
                tab_hop(h, True, b + 1, b + 2).start()

            tab_hop(h, False, 0, 31 - b).wait_recv()
            tab_down(h, 31 - b).start()

            tab_hop(h, False, 31 - b, 30 - b).start()

        @pl.when(b == 2)
        def _():
            for copy in panels_here:
                copy.wait()
            for copy in coming[4:]:
                copy.wait_recv()

        first = jnp.where(b < 3, 0, jnp.where(b < 4, 2, b))
        last = jnp.where(b < 2, 0, jnp.where(b < 3, 2, b + 1))

        for kg in range(2):
            for piece in range(CUTS):
                up_end, down_end = (15, 14) if kg == 0 else (14, 15)
                for h in range(2):
                    hop(h, True, b, b + 1, kg, piece).wait_recv()

                    @pl.when(b < up_end)
                    def _():
                        hop(h, True, b + 1, b + 2, kg, piece).start()

                    hop(h, False, 0, 31 - b, kg, piece).wait_recv()

                    @pl.when(b < down_end)
                    def _():
                        hop(h, False, 31 - b, 30 - b, kg, piece).start()

            @pl.loop(first, last)
            def _(i):
                if kg == 0:
                    for h in range(2):
                        tab_down(h, i).wait()
                        tab_down(h, 31 - i).wait()
                compute(i, kg, 0, 4)
                if kg == 0:
                    @pl.when(i >= 4)
                    def _():
                        finish(i - 4)
                else:
                    for r in (2, 1, 3):
                        reduce_copy(i, r).start()

    last_b = STEPS - 1
    for h in range(2):
        tab_hop(h, False, 0, STEPS).wait_recv()
        tab_down(h, STEPS).start()
    for h in range(2):
        tab_down(h, last_b).wait()
    for kg in range(2):
        compute(last_b, kg, 0, 2)
    for r in (2, 1, 3):
        half_copy(last_b, r, 0).start()
    finish(STEPS - 5)
    finish(STEPS - 4)
    for h in range(2):
        tab_down(h, STEPS).wait()
    for kg in range(2):
        for piece in range(CUTS):
            for h in range(2):
                hop(h, False, 0, STEPS, kg, piece).wait_recv()
        compute(last_b, kg, 2, 2)
        if kg == 0:
            finish(STEPS - 3)
    for r in (2, 1, 3):
        half_copy(last_b, r, 1).start()
    finish(STEPS - 2)
    finish(STEPS - 1)

    @pl.loop(0, STEPS)
    def _(b):
        share_copy(b, other).wait_recv()

    def final_copy(r):
        to = across[r]
        return pltpu.make_async_remote_copy(
            src_ref=fin_s.at[r], dst_ref=fin_r.at[r - 1], send_sem=fin_ss, recv_sem=fin_rs.at[r - 1],
            device_id=(2 * to + c, d), device_id_type=MESH)

    for r in (2, 1, 3, 0):
        to = across[r]
        for i in range(16):
            rows = total[loc[to * 16 + i]]
            fin_s[r, pl.ds(HALF * i, 16, stride=2)] = rows[:16]
            fin_s[r, pl.ds(HALF * i + 1, 16, stride=2)] = rows[16:]
        if r:
            final_copy(r).start()
    def columns(of):
        return pl.ds(pl.multiple_of(128 * of, 128), 128)

    base_here.wait()
    out[:, columns(x)] = base_v[:, columns(x)] + fin_s[0]

    def drain(ref, sem):
        pltpu.make_async_copy(ref, ref, sem).wait()

    for copy in going:
        copy.wait_send()
    for h in range(2):
        drain(held.at[h, pl.ds(0, 31)], ring_s.at[h])
        drain(tab_v.at[h, pl.ds(0, 31)], tab_ss.at[h])
    drain(got, red_s)
    drain(total.at[pl.ds(0, 4 * STEPS)], sh_s)

    for r in (1, 3, 2):
        final_copy(r).wait_recv()
        cols = columns(across[4 - r])
        out[:, cols] = base_v[:, cols] + fin_r[r - 1]
    drain(fin_r, fin_ss)


def per_device(
    ladder_amps, ladder_ids, ladder_count, cycle_amps, cycle_ids, cycle_count,
    ladder_panel, cycle_panel, owners, base,
):
    i32 = jnp.int32
    lad_amps, cyc_amps = ladder_amps.transpose(1, 0, 2), cycle_amps.transpose(1, 0, 2)
    lad_n, cyc_n = ladder_count.reshape(2), cycle_count.reshape(2)

    hbm = pl.BlockSpec(memory_space=pl.ANY)
    bf16, f32 = jnp.bfloat16, jnp.float32
    dma = pltpu.SemaphoreType.DMA
    summed = pl.pallas_call(
        kernel,
        name="ladder_ring",
        out_shape=jax.ShapeDtypeStruct((512, 512), f32),
        in_specs=[hbm] * 10,
        out_specs=pl.BlockSpec(memory_space=pltpu.VMEM),
        scratch_shapes=[
            pltpu.SMEM((2, KCAP_L), i32),
            pltpu.SMEM((2,), i32),
            pltpu.SMEM((2, KCAP_R), i32),
            pltpu.SMEM((2,), i32),
            pltpu.SMEM((64,), i32),
            pltpu.VMEM((KCAP_L, 2, TS * TS), bf16),
            pltpu.VMEM((KCAP_R, 2, TS * TS), bf16),
            pltpu.VMEM((2, 2, SLOTS, 16, 128), bf16),
            pltpu.VMEM((2, 32, 2, SLOTS, 16, 128), bf16),
            pltpu.VMEM((2, 1, 128), i32),
            pltpu.VMEM((2, 32, 2, 1, 128), i32),
            pltpu.SMEM((2, 32, 2, 1, 128), i32),
            pltpu.SMEM((64,), i32),
            pltpu.VMEM((2, 2048, 512), bf16),
            pltpu.VMEM((2 * VAR, 16, 128), bf16),
            pltpu.VMEM((128, 2048), bf16),
            pltpu.VMEM((STEPS, 4, 128, 128), f32),
            pltpu.VMEM((STEPS, 3, 128, 128), f32),
            pltpu.VMEM((2 * STEPS * 4, HALF, 128), f32),
            pltpu.VMEM((4, 512, 128), f32),
            pltpu.VMEM((3, 512, 128), f32),
            pltpu.VMEM((512, 512), f32),
            dma((10,)), dma((6,)), dma((6,)), dma((2,)), dma((2, 32)), dma((2, 32)),
            dma((2,)), dma((2, 32, 2, CUTS)),
            dma, dma((STEPS, 3)), dma, dma((STEPS,)), dma, dma((3,)),
        ],
        compiler_params=pltpu.CompilerParams(has_side_effects=True, collective_id=0, vmem_limit_bytes=58 * 2**20),
    )(lad_amps, cyc_amps, ladder_ids, lad_n, cycle_ids, cyc_n, owners, ladder_panel, cycle_panel, base)
    return summed


def solution(mesh):
    placed = (
        P("dev", "grp", None),
        P("dev", "grp"),
        P("dev", "grp"),
        P("dev", "grp", None),
        P("dev", "grp"),
        P("dev", "grp"),
        P("grp", "dev"),
        P("grp", "dev"),
        P(),
        P("grp", "dev"),
    )
    return jax.shard_map(
        per_device, mesh=mesh, in_specs=placed, out_specs=P("grp", "dev"), check_vma=False
    )
```

```python
import jax
import jax.numpy as jnp
from jax import lax
from jax.experimental import pallas as pl
from jax.experimental.pallas import tpu as pltpu
from jax.sharding import PartitionSpec as P

TS = 64
KLT = 24
KRT = 8
MESH = pl.DeviceIdType.MESH
STEPS = 16
HALF = 32
KCAP_L = 18
KCAP_R = 6
SLOTS = KCAP_L + KCAP_R
CUTS = 2
CUT = SLOTS // CUTS
ZERO = SLOTS
VAR = SLOTS + 1


def pos_first(z, y):
    return 4 * z + (y + z) % 4


def dev_first(s):
    k = s // 4
    return 4 * k + (s % 4 + 32 - k) % 4


def pos_second(z, y):
    t = (z + 24 - 3 * y) % 8
    return 4 * y + 16 * (t // 4) + t % 4


def dev_second(s):
    k = s // 4
    return 4 * ((3 * k + s % 4) % 8) + k % 4


POS = (pos_first, pos_second)
DEV = (dev_first, dev_second)


def kernel(
    lad_amps, cyc_amps, lad_ids_h, lad_n_h, cyc_ids_h, cyc_n_h, owners_h, lad, cyc, base, out,
    lad_ids, lad_n, cyc_ids, cyc_n, owners,
    amps_l, amps_c, own, held, tab_own, tab_v, tab_s, loc, panel, spread, lhs, part, got, total, fin_s, fin_r, base_v,
    local_sem, pair_s, pair_r, tab_ss, tab_rs, tab_ls, ring_s, ring_r,
    red_s, red_r, sh_s, sh_r, fin_ss, fin_rs,
):
    g = lax.axis_index("grp")
    d = lax.axis_index("dev")
    x = g // 2
    c = g % 2
    z = d // 4
    y = d % 4
    other = 1 - c
    mate = (2 * x + other, d)
    across = [(x + r) % 4 for r in range(4)]
    pos = [POS[h](z, y) for h in range(2)]
    nxt = [(g, DEV[h]((pos[h] + 1) % 32)) for h in range(2)]
    prv = [(g, DEV[h]((pos[h] + 31) % 32)) for h in range(2)]

    def local(i, src, dst):
        return pltpu.make_async_copy(src, dst, local_sem.at[i])

    def to_mate(i, src, dst):
        return pltpu.make_async_remote_copy(
            src_ref=src, dst_ref=dst, send_sem=pair_s.at[i], recv_sem=pair_r.at[i],
            device_id=mate, device_id_type=MESH)

    barrier = pltpu.get_barrier_semaphore()
    peers = nxt + prv + [mate] + [(2 * across[r] + c, d) for r in (1, 2, 3)]
    for p in peers:
        pl.semaphore_signal(barrier, inc=1, device_id=p, device_id_type=MESH)

    amps_here = [local(0, lad_amps, amps_l), local(1, cyc_amps, amps_c)]
    panels_here = [
        local(2, lad, panel.at[c, pl.ds(0, 1536)]),
        local(3, cyc, panel.at[c, pl.ds(1536, 512)]),
    ]
    base_here = local(4, base, base_v)
    lists_here = [
        local(5, lad_ids_h, lad_ids), local(6, lad_n_h, lad_n),
        local(7, cyc_ids_h, cyc_ids), local(8, cyc_n_h, cyc_n), local(9, owners_h, owners),
    ]
    for copy in amps_here + lists_here + panels_here + [base_here]:
        copy.start()
    for copy in lists_here:
        copy.wait()

    lane = lax.broadcasted_iota(jnp.int32, (1, 128), 1)
    for t in range(2):
        row = jnp.full((1, 128), ZERO, jnp.int32)
        for slot in range(KCAP_L + KCAP_R):
            if slot < KCAP_L:
                tile, live = lad_ids[t, slot], slot < lad_n[t]
            else:
                tile, live = cyc_ids[t, slot - KCAP_L] + KLT, slot - KCAP_L < cyc_n[t]
            row = jnp.where(lane == jnp.where(live, tile, -1), slot, row)
        tab_own[t] = row
    for copy in amps_here:
        copy.wait()
    for t in range(2):
        for amps, first, count in ((amps_l, 0, KCAP_L), (amps_c, KCAP_L, KCAP_R)):
            pairs = amps[:, t, :].reshape(count, HALF, 128)
            for h in range(2):
                own[t, h, first:first + count] = pairs[:, 16 * h:16 * (h + 1)]
    for h in range(2):
        held[h, 0, c] = own[c, h]
        tab_v[h, 0, c] = tab_own[c]

    pl.semaphore_wait(barrier, len(peers))

    def mates(side):
        return [
            to_mate(0, own.at[other, 0], held.at[0, 0, side]),
            to_mate(1, own.at[other, 1], held.at[1, 0, side]),
            to_mate(2, tab_own.at[other], tab_v.at[0, 0, side]),
            to_mate(3, tab_own.at[other], tab_v.at[1, 0, side]),
            to_mate(4, lad, panel.at[side, pl.ds(0, 1536)]),
            to_mate(5, cyc, panel.at[side, pl.ds(1536, 512)]),
        ]

    going = mates(c)
    coming = mates(other)
    for copy in going:
        copy.start()

    def hop(h, up, src, dst, kg, piece):
        rows = pl.ds(CUT * piece, CUT)
        return pltpu.make_async_remote_copy(
            src_ref=held.at[h, src, kg, rows], dst_ref=held.at[h, dst, kg, rows],
            send_sem=ring_s.at[h], recv_sem=ring_r.at[h, dst, kg, piece],
            device_id=nxt[h] if up else prv[h], device_id_type=MESH)

    def tab_hop(h, up, src, dst):
        return pltpu.make_async_remote_copy(
            src_ref=tab_v.at[h, src], dst_ref=tab_v.at[h, dst],
            send_sem=tab_ss.at[h], recv_sem=tab_rs.at[h, dst],
            device_id=nxt[h] if up else prv[h], device_id_type=MESH)

    def tab_down(h, slot):
        return pltpu.make_async_copy(tab_v.at[h, slot], tab_s.at[h, slot], tab_ls.at[h, slot])

    for piece in range(CUTS):
        for h in range(2):
            hop(h, True, 0, 1, c, piece).start()
            hop(h, False, 0, 31, c, piece).start()
    for h in range(2):
        coming[2 + h].wait_recv()
        tab_hop(h, True, 0, 1).start()
        tab_hop(h, False, 0, 31).start()
        tab_down(h, 0).start()
    for h in range(2):
        coming[h].wait_recv()
        for piece in range(CUTS):
            hop(h, True, 0, 1, other, piece).start()
            hop(h, False, 0, 31, other, piece).start()

    spread[ZERO] = jnp.zeros((16, 128), jnp.bfloat16)
    spread[VAR + ZERO] = jnp.zeros((16, 128), jnp.bfloat16)

    def seat(h, row, col):
        if h == 0:
            return 4 * row + ((col + row) & 3)
        t = (row + 24 - 3 * col) & 7
        return 4 * col + 16 * (t >> 2) + (t & 3)

    @pl.loop(0, 4)
    def _(to):
        for i in range(8):
            tile = owners[16 * to + 8 * c + i]
            row, col = tile >> 3, (tile >> 1) & 3
            for h in range(2):
                m = (pos[h] + 32 - seat(h, row, col)) & 31
                near = m < STEPS
                b = jnp.where(near, m, 31 - m)
                q = jnp.where(near, h, 2 + h)
                loc[16 * to + 2 * i + h] = 4 * (STEPS * (tile & 1) + b) + q

    left = lax.broadcasted_iota(jnp.int32, (16, 128), 1) < 64

    def reduce_copy(b, r):
        to = across[r]
        return pltpu.make_async_remote_copy(
            src_ref=part.at[b, to], dst_ref=got.at[b, r - 1],
            send_sem=red_s, recv_sem=red_r.at[b, r - 1],
            device_id=(2 * to + c, d), device_id_type=MESH)

    def half_copy(b, r, half):
        to = across[r]
        rows = pl.ds(64 * half, 64)
        return pltpu.make_async_remote_copy(
            src_ref=part.at[b, to, rows], dst_ref=got.at[b, r - 1, rows],
            send_sem=red_s, recv_sem=red_r.at[b, r - 1],
            device_id=(2 * to + c, d), device_id_type=MESH)

    def share_copy(b, side):
        rows = total.at[pl.ds((side * STEPS + b) * 4, 4)]
        return pltpu.make_async_remote_copy(
            src_ref=rows, dst_ref=rows, send_sem=sh_s, recv_sem=sh_r.at[b],
            device_id=mate, device_id_type=MESH)

    def finish(b):
        for r in (1, 2, 3):
            reduce_copy(b, r).wait_recv()
        s = part[b, x] + got[b, 0] + got[b, 1] + got[b, 2]
        for q in range(4):
            total[(c * STEPS + b) * 4 + q] = s[HALF * q:HALF * (q + 1)]
        share_copy(b, c).start()

    def compute(b, kg, first, count):
        for n in range(count):
            q = first + n
            h = q % 2
            m = b if q < 2 else 31 - b
            for p in range(SLOTS):
                v = held[h, m, kg, p]
                spread[p] = v
                spread[VAR + p] = jnp.concatenate([v[:, 64:], v[:, :64]], axis=1)
            for j in range(16):
                a = tab_s[h, m, kg, 0, 2 * j]
                e = tab_s[h, m, kg, 0, 2 * j + 1]
                at = slice(128 * j, 128 * (j + 1))
                lhs[HALF * n:HALF * n + 16, at] = jnp.where(left, spread[a], spread[VAR + e])
                lhs[HALF * n + 16:HALF * (n + 1), at] = jnp.where(left, spread[VAR + a], spread[e])
        prod = jnp.dot(lhs[:HALF * count], panel[kg], preferred_element_type=jnp.float32)
        at = slice(HALF * first, HALF * (first + count))
        for q in range(4):
            piece = prod[:, 128 * q:128 * (q + 1)]
            part[b, q, at] = piece if kg == 0 else part[b, q, at] + piece

    @pl.loop(0, STEPS - 1)
    def _(b):
        for h in range(2):
            tab_hop(h, True, b, b + 1).wait_recv()
            tab_down(h, b + 1).start()

            @pl.when(b < 14)
            def _():
                tab_hop(h, True, b + 1, b + 2).start()

            tab_hop(h, False, 0, 31 - b).wait_recv()
            tab_down(h, 31 - b).start()

            tab_hop(h, False, 31 - b, 30 - b).start()

        @pl.when(b == 2)
        def _():
            for copy in panels_here:
                copy.wait()
            for copy in coming[4:]:
                copy.wait_recv()

        first = jnp.where(b < 3, 0, jnp.where(b < 4, 2, b))
        last = jnp.where(b < 2, 0, jnp.where(b < 3, 2, b + 1))

        for kg in range(2):
            for piece in range(CUTS):
                up_end, down_end = (15, 14) if kg == 0 else (14, 15)
                for h in range(2):
                    hop(h, True, b, b + 1, kg, piece).wait_recv()

                    @pl.when(b < up_end)
                    def _():
                        hop(h, True, b + 1, b + 2, kg, piece).start()

                    hop(h, False, 0, 31 - b, kg, piece).wait_recv()

                    @pl.when(b < down_end)
                    def _():
                        hop(h, False, 31 - b, 30 - b, kg, piece).start()

            @pl.loop(first, last)
            def _(i):
                if kg == 0:
                    for h in range(2):
                        tab_down(h, i).wait()
                        tab_down(h, 31 - i).wait()
                compute(i, kg, 0, 4)
                if kg == 0:
                    @pl.when(i >= 4)
                    def _():
                        finish(i - 4)
                else:
                    for r in (1, 3, 2):
                        reduce_copy(i, r).start()

    last_b = STEPS - 1
    for h in range(2):
        tab_hop(h, False, 0, STEPS).wait_recv()
        tab_down(h, STEPS).start()
    for h in range(2):
        tab_down(h, last_b).wait()
    for kg in range(2):
        compute(last_b, kg, 0, 2)
    for r in (1, 3, 2):
        half_copy(last_b, r, 0).start()
    finish(STEPS - 5)
    finish(STEPS - 4)
    for h in range(2):
        tab_down(h, STEPS).wait()
    for kg in range(2):
        for piece in range(CUTS):
            for h in range(2):
                hop(h, False, 0, STEPS, kg, piece).wait_recv()
        compute(last_b, kg, 2, 2)
        if kg == 0:
            finish(STEPS - 3)
    for r in (1, 3, 2):
        half_copy(last_b, r, 1).start()
    finish(STEPS - 2)
    finish(STEPS - 1)

    @pl.loop(0, STEPS)
    def _(b):
        share_copy(b, other).wait_recv()

    def final_copy(r):
        to = across[r]
        return pltpu.make_async_remote_copy(
            src_ref=fin_s.at[r], dst_ref=fin_r.at[r - 1], send_sem=fin_ss, recv_sem=fin_rs.at[r - 1],
            device_id=(2 * to + c, d), device_id_type=MESH)

    for r in (2, 1, 3, 0):
        to = across[r]
        for i in range(16):
            rows = total[loc[to * 16 + i]]
            fin_s[r, pl.ds(HALF * i, 16, stride=2)] = rows[:16]
            fin_s[r, pl.ds(HALF * i + 1, 16, stride=2)] = rows[16:]
        if r:
            final_copy(r).start()
    def columns(of):
        return pl.ds(pl.multiple_of(128 * of, 128), 128)

    base_here.wait()
    out[:, columns(x)] = base_v[:, columns(x)] + fin_s[0]

    def drain(ref, sem):
        pltpu.make_async_copy(ref, ref, sem).wait()

    for copy in going:
        copy.wait_send()
    for h in range(2):
        drain(held.at[h, pl.ds(0, 31)], ring_s.at[h])
        drain(tab_v.at[h, pl.ds(0, 31)], tab_ss.at[h])
    drain(got, red_s)
    drain(total.at[pl.ds(0, 4 * STEPS)], sh_s)

    for r in (1, 3, 2):
        final_copy(r).wait_recv()
        cols = columns(across[4 - r])
        out[:, cols] = base_v[:, cols] + fin_r[r - 1]
    drain(fin_r, fin_ss)


def per_device(
    ladder_amps, ladder_ids, ladder_count, cycle_amps, cycle_ids, cycle_count,
    ladder_panel, cycle_panel, owners, base,
):
    i32 = jnp.int32
    lad_amps, cyc_amps = ladder_amps.transpose(1, 0, 2), cycle_amps.transpose(1, 0, 2)
    lad_n, cyc_n = ladder_count.reshape(2), cycle_count.reshape(2)

    hbm = pl.BlockSpec(memory_space=pl.ANY)
    bf16, f32 = jnp.bfloat16, jnp.float32
    dma = pltpu.SemaphoreType.DMA
    summed = pl.pallas_call(
        kernel,
        name="ladder_ring",
        out_shape=jax.ShapeDtypeStruct((512, 512), f32),
        in_specs=[hbm] * 10,
        out_specs=pl.BlockSpec(memory_space=pltpu.VMEM),
        scratch_shapes=[
            pltpu.SMEM((2, KCAP_L), i32),
            pltpu.SMEM((2,), i32),
            pltpu.SMEM((2, KCAP_R), i32),
            pltpu.SMEM((2,), i32),
            pltpu.SMEM((64,), i32),
            pltpu.VMEM((KCAP_L, 2, TS * TS), bf16),
            pltpu.VMEM((KCAP_R, 2, TS * TS), bf16),
            pltpu.VMEM((2, 2, SLOTS, 16, 128), bf16),
            pltpu.VMEM((2, 32, 2, SLOTS, 16, 128), bf16),
            pltpu.VMEM((2, 1, 128), i32),
            pltpu.VMEM((2, 32, 2, 1, 128), i32),
            pltpu.SMEM((2, 32, 2, 1, 128), i32),
            pltpu.SMEM((64,), i32),
            pltpu.VMEM((2, 2048, 512), bf16),
            pltpu.VMEM((2 * VAR, 16, 128), bf16),
            pltpu.VMEM((128, 2048), bf16),
            pltpu.VMEM((STEPS, 4, 128, 128), f32),
            pltpu.VMEM((STEPS, 3, 128, 128), f32),
            pltpu.VMEM((2 * STEPS * 4, HALF, 128), f32),
            pltpu.VMEM((4, 512, 128), f32),
            pltpu.VMEM((3, 512, 128), f32),
            pltpu.VMEM((512, 512), f32),
            dma((10,)), dma((6,)), dma((6,)), dma((2,)), dma((2, 32)), dma((2, 32)),
            dma((2,)), dma((2, 32, 2, CUTS)),
            dma, dma((STEPS, 3)), dma, dma((STEPS,)), dma, dma((3,)),
        ],
        compiler_params=pltpu.CompilerParams(has_side_effects=True, collective_id=0, vmem_limit_bytes=58 * 2**20),
    )(lad_amps, cyc_amps, ladder_ids, lad_n, cycle_ids, cyc_n, owners, ladder_panel, cycle_panel, base)
    return summed


def solution(mesh):
    placed = (
        P("dev", "grp", None),
        P("dev", "grp"),
        P("dev", "grp"),
        P("dev", "grp", None),
        P("dev", "grp"),
        P("dev", "grp"),
        P("grp", "dev"),
        P("grp", "dev"),
        P(),
        P("grp", "dev"),
    )
    return jax.shard_map(
        per_device, mesh=mesh, in_specs=placed, out_specs=P("grp", "dev"), check_vma=False
    )
```
